256 devices in a mesh: blk: 64 (over x, y_lo, z), heads: 4 (over y_hi, core).
Axes of the slice: x: 4, y: 4 (y_hi: 2, y_lo: 2; y = y_hi * 2 + y_lo), z: 8, core: 2. Of those that a mesh axis runs over, the one named last changes fastest.
Arguments:
- queries: float32 [4096, 8192], P('blk', 'heads'), may hold values from -6 to 6
- visual_keys: float32 [65536, 1024], P('blk', 'heads'), may hold values from -6 to 6
- projected_values: float32 [65536, 1024], P('blk', 'heads'), may hold values from -6 to 6
- valid_lengths: int32 [64], P('blk'), may hold values from 256 to 1024, as said below
Outputs:
- attended: float32 [4096, 8192], P('blk', 'heads')
The draws below stay inside these ranges and needn't reach their ends.
Inputs may be any that keep to these rules, and one draw needn't show every extreme that they name: `valid_lengths`: some block has all 1024 tokens valid in every draw.
All inputs are finite; a program needn't handle non-finite values.
Results may differ from the reference program's by a relative error of at most 0.0003.
Values sent between devices are 32-bit elements; how exact they have to be, the bound alone decides.
No kernel may reach another device: no remote copies, remote signals or barrier semaphores. Data moves between devices by JAX's collectives and lax.ppermute only.
A program may use at most 64 MiB of HBM per device.

```python
import jax
import jax.numpy as jnp
from jax import lax

QH = 64
KEY_VALUE_HEADS = 8
HEAD_DIM = 128
QB = 64
BLOCK_TOKENS = 1024
WIN = 6
NQ = 4096
TOTAL_TOKENS = 65536


def draw_queries(key, part):
    local_key = jax.random.fold_in(key, 3)
    return jnp.clip(1.6 * jax.random.normal(local_key, (NQ, QH * HEAD_DIM), jnp.float32), -6.0, 6.0)


def draw_visual_keys(key, part):
    local_key = jax.random.fold_in(key, 7)
    return jnp.clip(1.6 * jax.random.normal(local_key, (TOTAL_TOKENS, KEY_VALUE_HEADS * HEAD_DIM), jnp.float32), -6.0, 6.0)


def draw_valid_lengths(key, part):
    shard_blocks = TOTAL_TOKENS // BLOCK_TOKENS
    picks = jax.random.randint(jax.random.fold_in(key, 23), (shard_blocks,), BLOCK_TOKENS // 4, BLOCK_TOKENS + 1)
    chosen = jax.random.randint(jax.random.fold_in(key, 29), (), 0, shard_blocks)
    return jnp.where(jnp.arange(shard_blocks) == chosen, BLOCK_TOKENS, picks).astype(jnp.int32)


def shard_levels(key, dims, split, least, top_value):
    def one(axis_at, shards_of):
        steps = jax.random.uniform(jax.random.fold_in(jax.random.fold_in(key, 6), axis_at), (shards_of,), jnp.float32, least / len(split), top_value / len(split))
        return jnp.repeat(jnp.exp(steps), dims[axis_at] // shards_of).reshape((-1,) + (1,) * (len(dims) - axis_at - 1))

    gain = one(*split[0])
    for cut in split[1:]:
        gain = gain * one(*cut)
    return gain


def scatter_about(stream_key, extent, scale, limit, pieces=(), kind=jnp.bfloat16):
    drawn = scale * jax.random.normal(stream_key, extent, jnp.float32)
    if pieces:
        drawn = drawn * shard_levels(stream_key, extent, pieces, -0.22, 0.18)
    return jnp.clip(drawn, -limit, limit).astype(kind)


def setup_inputs(seed: int = 0) -> dict:
    key_list = jax.random.split(jax.random.key(seed), 5)
    queries = draw_queries(jax.random.fold_in(key_list[4], 71), 0)
    visual_keys = draw_visual_keys(jax.random.fold_in(key_list[4], 71), 0)
    projected_values = scatter_about(key_list[2], (TOTAL_TOKENS, KEY_VALUE_HEADS * HEAD_DIM), 1.0, 6.0, ((0, 64), (1, 4)), jnp.float32)
    valid_lengths = draw_valid_lengths(jax.random.fold_in(key_list[4], 71), 0)
    return {"queries": queries, "visual_keys": visual_keys, "projected_values": projected_values, "valid_lengths": valid_lengths}


def reference(queries, visual_keys, projected_values, valid_lengths):
    shard_blocks = TOTAL_TOKENS // BLOCK_TOKENS
    left_reach = WIN // 2 - 1
    right_reach = WIN // 2
    group_size = QH // KEY_VALUE_HEADS
    scaled = queries * (HEAD_DIM ** -0.5)
    key_blocks = jnp.pad(visual_keys.reshape(shard_blocks, BLOCK_TOKENS, KEY_VALUE_HEADS, HEAD_DIM), ((left_reach, right_reach), (0, 0), (0, 0), (0, 0)))
    value_blocks = jnp.pad(projected_values.reshape(shard_blocks, BLOCK_TOKENS, KEY_VALUE_HEADS, HEAD_DIM), ((left_reach, right_reach), (0, 0), (0, 0), (0, 0)))
    counts = jnp.pad(valid_lengths, (left_reach, right_reach))
    positions = jnp.arange(BLOCK_TOKENS, dtype=jnp.int32)

    def one_block(block_index):
        query_tile = lax.dynamic_slice_in_dim(scaled, block_index * QB, QB, 0).reshape(QB, KEY_VALUE_HEADS, group_size, HEAD_DIM)
        window_keys = lax.dynamic_slice_in_dim(key_blocks, block_index, WIN, 0).reshape(WIN * BLOCK_TOKENS, KEY_VALUE_HEADS, HEAD_DIM)
        window_values = lax.dynamic_slice_in_dim(value_blocks, block_index, WIN, 0).reshape(WIN * BLOCK_TOKENS, KEY_VALUE_HEADS, HEAD_DIM)
        window_counts = lax.dynamic_slice_in_dim(counts, block_index, WIN, 0)
        usable = (positions[None, :] < window_counts[:, None]).reshape(WIN * BLOCK_TOKENS)
        scores = jnp.einsum("qhgd,khd->hgqk", query_tile, window_keys, precision=lax.Precision.HIGHEST)
        scores = jnp.where(usable, scores, -jnp.inf)
        peak_score = jnp.max(scores, axis=-1, keepdims=True)
        weights = jnp.exp(scores - peak_score)
        weight_sum = jnp.sum(weights, axis=-1)
        numerator = jnp.einsum("hgqk,khd->qhgd", weights, window_values, precision=lax.Precision.HIGHEST)
        return (numerator / jnp.transpose(weight_sum, (2, 0, 1))[..., None]).reshape(QB, QH * HEAD_DIM)

    blocks = lax.map(one_block, jnp.arange(shard_blocks, dtype=jnp.int32))
    return blocks.reshape(NQ, QH * HEAD_DIM)
```

```python
import functools
import jax
import jax.numpy as jnp
from jax import lax
from jax.experimental import pallas as pl
from jax.experimental.pallas import tpu as pltpu
from jax.sharding import PartitionSpec as P

HEAD_DIM = 128
LOG2E = 1.4426950408889634
LOW = -1e30
CHUNK = 256
LANES = 128
GROUP = 8


def split(x):
    high = x.astype(jnp.bfloat16)
    return high, (x - high.astype(jnp.float32)).astype(jnp.bfloat16)


def query_side(q_ref, h):
    parts = []
    for g in range(h * GROUP, (h + 1) * GROUP):
        high, low = split(q_ref[:, g * HEAD_DIM:(g + 1) * HEAD_DIM] * (HEAD_DIM ** -0.5 * LOG2E))
        parts.append(jnp.concatenate([high, low, high, low], axis=1))
    return jnp.concatenate(parts, axis=0)


def attend(count, q_side, key_chunk, value_chunk, blocks, scores_ref, store):
    width = q_side.shape[0]
    top = jnp.full((8, width), LOW, jnp.float32)
    for c in range(blocks):
        high, low = key_chunk(c)
        k_side = jnp.concatenate([high, high, low, low], axis=1)
        s = lax.dot_general(k_side, q_side, (((1,), (1,)), ((), ())), preferred_element_type=jnp.float32)
        row = lax.broadcasted_iota(jnp.int32, (CHUNK, width), 0) + c * CHUNK
        s = jnp.where(row < count, s, LOW)
        scores_ref[c * CHUNK:(c + 1) * CHUNK, :] = s
        top = jnp.maximum(top, jnp.max(s.reshape(CHUNK // 8, 8, width), axis=0))
    peak = jnp.max(top, axis=0, keepdims=True)
    total = jnp.zeros((8, width), jnp.float32)
    acc = None
    for c in range(blocks):
        p = jnp.exp2(scores_ref[c * CHUNK:(c + 1) * CHUNK, :] - peak)
        total = total + jnp.sum(p.reshape(CHUNK // 8, 8, width), axis=0)
        p_high, p_low = split(p)
        sides = value_chunk(c)
        both = jnp.dot(sides, p_high, preferred_element_type=jnp.float32)
        term = both[:HEAD_DIM] + both[HEAD_DIM:] + jnp.dot(sides[:HEAD_DIM], p_low, preferred_element_type=jnp.float32)
        acc = term if acc is None else acc + term
    store(acc, peak, jnp.sum(total, axis=0, keepdims=True))


def store_part(out_ref, i, acc, peak, mass):
    tiles = acc.shape[1] // LANES
    base = tiles * HEAD_DIM
    for j in range(tiles):
        lanes = slice(j * LANES, (j + 1) * LANES)
        out_ref[i, j * HEAD_DIM:(j + 1) * HEAD_DIM, :] = acc[:, lanes]
        out_ref[i, base + j:base + j + 1, :] = peak[:, lanes]
        out_ref[i, base + tiles + j:base + tiles + j + 1, :] = mass[:, lanes]


def side_chunks(k_sides_ref, v_sides_ref, h):
    def keys(c):
        rows = slice(c * CHUNK, (c + 1) * CHUNK)
        return k_sides_ref[h, rows, :HEAD_DIM], k_sides_ref[h, rows, HEAD_DIM:]

    def values(c):
        return v_sides_ref[h, :, c * CHUNK:(c + 1) * CHUNK]

    return keys, values


def own_kernel(info_ref, q_ref, k_ref, v_ref, out_ref, k_sides_ref, v_sides_ref, scores_ref):
    blocks = k_ref.shape[0] // CHUNK
    for h in range(out_ref.shape[0]):
        cols = slice(h * HEAD_DIM, (h + 1) * HEAD_DIM)
        for c in range(blocks):
            rows = slice(c * CHUNK, (c + 1) * CHUNK)
            high, low = split(k_ref[rows, cols])
            k_sides_ref[h, rows, :HEAD_DIM] = high
            k_sides_ref[h, rows, HEAD_DIM:] = low
            high, low = split(v_ref[rows, cols].T)
            v_sides_ref[h, :HEAD_DIM, rows] = high
            v_sides_ref[h, HEAD_DIM:, rows] = low
        attend(info_ref[1], query_side(q_ref, h), *side_chunks(k_sides_ref, v_sides_ref, h), blocks, scores_ref,
               functools.partial(store_part, out_ref, h))


WHOLE = pl.BlockSpec(memory_space=pltpu.VMEM)


def own_visit(info, q, keys, values):
    rows = keys.shape[0]
    n = keys.shape[1] // HEAD_DIM
    width = q.shape[0] * GROUP
    tall = (width // LANES) * (HEAD_DIM + 2)
    return pl.pallas_call(
        own_kernel,
        in_specs=[pl.BlockSpec(memory_space=pltpu.SMEM), WHOLE, WHOLE, WHOLE],
        out_specs=(WHOLE, WHOLE, WHOLE),
        out_shape=(
            jax.ShapeDtypeStruct((n, tall, LANES), jnp.float32),
            jax.ShapeDtypeStruct((n, rows, 2 * HEAD_DIM), jnp.bfloat16),
            jax.ShapeDtypeStruct((n, 2 * HEAD_DIM, rows), jnp.bfloat16),
        ),
        scratch_shapes=[pltpu.VMEM((rows, width), jnp.float32)],
        cost_estimate=pl.CostEstimate(flops=n * 12 * width * rows * HEAD_DIM, bytes_accessed=n * 2**20 * 2, transcendentals=n * width * rows),
        compiler_params=pltpu.CompilerParams(vmem_limit_bytes=14 * 2**20),
    )(info, q, keys, values)


def visit_kernel(heads, q_heads, info_ref, q_ref, k_sides_ref, v_sides_ref, out_ref, scores_ref):
    usable = info_ref[0]
    tiles = scores_ref.shape[1] // LANES

    @pl.when(usable > 0)
    def _():
        for i, (h, q_h) in enumerate(zip(heads, q_heads)):
            attend(info_ref[1], query_side(q_ref, q_h), *side_chunks(k_sides_ref, v_sides_ref, h),
                   scores_ref.shape[0] // CHUNK, scores_ref, functools.partial(store_part, out_ref, i))

    @pl.when(usable <= 0)
    def _():
        which = lax.broadcasted_iota(jnp.int32, (2 * tiles, LANES), 0)
        for i in range(len(heads)):
            out_ref[i, :tiles * HEAD_DIM, :] = jnp.zeros((tiles * HEAD_DIM, LANES), jnp.float32)
            out_ref[i, tiles * HEAD_DIM:, :] = jnp.where(which < tiles, LOW, 0.0)


def visit(info, q, sides, heads, q_heads):
    k_sides, v_sides = sides
    n = len(heads)
    rows = k_sides.shape[1]
    width = q.shape[0] * GROUP
    tall = (width // LANES) * (HEAD_DIM + 2)
    return pl.pallas_call(
        functools.partial(visit_kernel, heads, q_heads),
        in_specs=[pl.BlockSpec(memory_space=pltpu.SMEM), WHOLE, WHOLE, WHOLE],
        out_specs=WHOLE,
        out_shape=jax.ShapeDtypeStruct((n, tall, LANES), jnp.float32),
        scratch_shapes=[pltpu.VMEM((rows, width), jnp.float32)],
        cost_estimate=pl.CostEstimate(flops=n * 12 * width * rows * HEAD_DIM, bytes_accessed=2**20 * 2, transcendentals=n * width * rows),
        compiler_params=pltpu.CompilerParams(vmem_limit_bytes=10 * 2**20),
    )(info, q, k_sides, v_sides)


def combined(parts, j, tiles):
    base = tiles * HEAD_DIM
    peaks = [r[i, base + j:base + j + 1, :] for r, i in parts]
    peak = functools.reduce(jnp.maximum, peaks)
    acc = 0.0
    mass = 0.0
    for (r, i), one in zip(parts, peaks):
        factor = jnp.exp2(one - peak)
        acc = acc + r[i, j * HEAD_DIM:(j + 1) * HEAD_DIM, :] * factor
        mass = mass + r[i, base + tiles + j:base + tiles + j + 1, :] * factor
    return peak, acc, mass


def merge_kernel(first, a_ref, b_ref, out_ref):
    n, tall, _ = out_ref.shape
    tiles = tall // (HEAD_DIM + 2)
    base = tiles * HEAD_DIM
    for i in range(n):
        for j in range(tiles):
            peak, acc, mass = combined(((a_ref, first + i), (b_ref, i)), j, tiles)
            out_ref[i, j * HEAD_DIM:(j + 1) * HEAD_DIM, :] = acc
            out_ref[i, base + j:base + j + 1, :] = peak
            out_ref[i, base + tiles + j:base + tiles + j + 1, :] = mass


def merge(a, b, first=0):
    n, tall, lanes = b.shape
    return pl.pallas_call(
        functools.partial(merge_kernel, first),
        in_specs=[WHOLE, WHOLE],
        out_specs=WHOLE,
        out_shape=jax.ShapeDtypeStruct(b.shape, jnp.float32),
        cost_estimate=pl.CostEstimate(flops=3 * n * tall * lanes, bytes_accessed=12 * n * tall * lanes, transcendentals=0),
        compiler_params=pltpu.CompilerParams(vmem_limit_bytes=4 * 2**20),
    )(a, b)


def finish_kernel(own_ref, left_ref, right_a_ref, right_b_ref, out_ref):
    tiles = own_ref.shape[1] // (HEAD_DIM + 2)
    tokens = out_ref.shape[0]
    per = LANES // tokens
    for i, right_ref in enumerate((right_a_ref, right_b_ref)):
        for j in range(tiles):
            _, acc, mass = combined(((own_ref, i), (left_ref, i), (right_ref, 0)), j, tiles)
            normed = (acc / mass).T
            for g in range(per):
                head = (i * tiles + j) * per + g
                out_ref[:, head * HEAD_DIM:(head + 1) * HEAD_DIM] = normed[g * tokens:(g + 1) * tokens, :]


def finish(own, left, right_a, right_b, shape):
    return pl.pallas_call(
        finish_kernel,
        in_specs=[WHOLE] * 4,
        out_specs=WHOLE,
        out_shape=jax.ShapeDtypeStruct(shape, jnp.float32),
        cost_estimate=pl.CostEstimate(flops=10 * own.size, bytes_accessed=16 * own.size, transcendentals=0),
        compiler_params=pltpu.CompilerParams(vmem_limit_bytes=8 * 2**20),
    )(own, left, right_a, right_b)


def shift(x, by):
    size = lax.axis_size("blk")
    return lax.ppermute(x, "blk", [(i, (i + by) % size) for i in range(size)])


def per_device(queries, visual_keys, projected_values, valid_lengths):
    size = lax.axis_size("blk")
    here = lax.axis_index("blk")
    half = queries.shape[1] // 2

    def info(offset):
        query_block = here - offset
        fits = (query_block >= 0) & (query_block < size)
        return jnp.stack([fits.astype(jnp.int32), valid_lengths[0]])

    def look(q, offset, heads=(0, 1), q_heads=(0, 1)):
        return visit(info(offset), q, sides, heads, q_heads)

    f1 = shift(queries, 1)
    g1 = shift(queries, -1)
    own, *sides = own_visit(info(0), queries, visual_keys, projected_values)
    f2 = shift(f1, 1)
    g2 = shift(g1, -1)
    cf1 = look(f1, 1)
    cg1 = look(g1, -1)
    f3a = shift(f2[:, :half], 1)
    f3b = shift(f2[:, half:], 1)
    cg2 = look(g2, -2)
    r2 = shift(cg2, 1)
    cf2a = look(f2, 2, (0,), (0,))
    cf3a = look(f3a, 3, (0,), (0,))
    s3a = shift(cf3a, -1)
    cf2b = look(f2, 2, (1,), (1,))
    cf3b = look(f3b, 3, (1,), (0,))
    s3b = shift(cf3b, -1)
    s2a = shift(merge(cf2a, s3a), -1)
    r1 = shift(merge(cg1, r2), 1)
    s2b = shift(merge(cf2b, s3b), -1)
    s1a = shift(merge(cf1, s2a, 0), -1)
    s1b = shift(merge(cf1, s2b, 1), -1)
    return finish(own, r1, s1a, s1b, queries.shape)


def solution(mesh):
    return jax.shard_map(
        per_device,
        mesh=mesh,
        in_specs=(P("blk", "heads"), P("blk", "heads"), P("blk", "heads"), P("blk")),
        out_specs=P("blk", "heads"),
        check_vma=False,
    )
```
